32 devices in a mesh: grp: 1, row: 8 (over z, y), col: 2 (over x), ch: 2 (over core).
Axes of the slice: x: 2, y: 2, z: 4, core: 2. Of those that a mesh axis runs over, the one named last changes fastest.
Arguments:
- pair_input: float32 [96, 96, 128], P(('grp', 'row'), ('col', 'ch')), may hold values from -6 to 6
- saved_product: float32 [96, 96, 128], P(('grp', 'row'), ('col', 'ch')), may hold values from -6 to 6
- pair_grad: float32 [96, 96, 128], P(('grp', 'row'), ('col', 'ch')), may hold values from -6 to 6
- token_mask: int32 [96], P('grp'), may hold values 0 or 1
- w_one: float32 [128, 512], replicated, may hold values from -0.5 to 0.5
- w_two: float32 [128, 512], replicated, may hold values from -0.5 to 0.5
- w_three: float32 [512, 128], replicated, may hold values from -0.25 to 0.25
- w_left: float32 [128, 128], replicated, may hold values from -0.5 to 0.5
- w_left_gate: float32 [128, 128], replicated, may hold values from -0.5 to 0.5
- w_right: float32 [128, 128], replicated, may hold values from -0.5 to 0.5
- w_right_gate: float32 [128, 128], replicated, may hold values from -0.5 to 0.5
- w_out: float32 [128, 128], replicated, may hold values from -0.5 to 0.5
- w_out_gate: float32 [128, 128], replicated, may hold values from -0.5 to 0.5
Outputs:
- input_grad: float32 [96, 96, 128], P(('grp', 'row'), ('col', 'ch'))
The draws below stay inside these ranges and needn't reach their ends.
All inputs are finite; a program needn't handle non-finite values.
Results may differ from the reference program's by a relative error of at most 0.0038.
Values may be sent and summed in bfloat16 or wider, within the bound.
A program may use at most 128 MiB of HBM per device.

```python
import jax
import jax.numpy as jnp
from jax import lax

CH = 128
HID = 512
TOKENS = 96


def with_ends(values, stream_key, low, top_value):
    spot = [jax.random.randint(jax.random.fold_in(stream_key, axis), (), 0, length) for axis, length in enumerate(values.shape)]
    widest = values.shape.index(max(values.shape))
    neighbour = spot[:widest] + [(spot[widest] + 1) % values.shape[widest]] + spot[widest + 1:]
    return values.at[tuple(spot)].set(low).at[tuple(neighbour)].set(top_value)


def level_of(key, dims, pieces, smallest, largest):
    gain, own = 1.0, jax.random.fold_in(key, 6)
    for dim, parts in pieces:
        heights = jnp.exp(jax.random.uniform(jax.random.fold_in(own, dim), (parts,), jnp.float32, smallest / len(pieces), largest / len(pieces)))
        gain = gain * jnp.repeat(heights, dims[dim] // parts).reshape([-1 if axis == dim else 1 for axis in range(len(dims))])
    return gain


def scatter_about(stream_key, dims, width, bound, cuts=(), kind=jnp.bfloat16):
    values = jax.random.normal(stream_key, dims, jnp.float32) * width
    if len(cuts) > 0:
        values = level_of(stream_key, dims, cuts, -0.22, 0.18) * values
    return jnp.clip(values, min=-bound, max=bound).astype(kind)


def setup_inputs(seed: int = 0, part: int = 0) -> dict:
    keys = jax.random.split(jax.random.key(seed), 14)
    part_splits = jax.random.split(jax.random.fold_in(keys[13], part), 14)
    return {
        "pair_input": scatter_about(part_splits[0], (TOKENS, TOKENS, CH), 1.0, 6.0, ((0, 8), (1, 4)), jnp.float32),
        "saved_product": scatter_about(part_splits[1], (TOKENS, TOKENS, CH), 1.0, 6.0, ((0, 8), (1, 4)), jnp.float32),
        "pair_grad": scatter_about(part_splits[2], (TOKENS, TOKENS, CH), 1.0, 6.0, ((0, 8), (1, 4)), jnp.float32),
        "token_mask": with_ends((jax.random.randint(part_splits[3], (TOKENS,), 0, 8) < 7).astype(jnp.int32), jax.random.fold_in(part_splits[3], 1), 0, 1),
        "w_one": scatter_about(keys[4], (CH, HID), CH ** -0.5, 0.5, (), jnp.float32),
        "w_two": scatter_about(keys[5], (CH, HID), CH ** -0.5, 0.5, (), jnp.float32),
        "w_three": scatter_about(keys[6], (HID, CH), HID ** -0.5, 0.25, (), jnp.float32),
        "w_left": scatter_about(keys[7], (CH, CH), CH ** -0.5, 0.5, (), jnp.float32),
        "w_left_gate": scatter_about(keys[8], (CH, CH), CH ** -0.5, 0.5, (), jnp.float32),
        "w_right": scatter_about(keys[9], (CH, CH), CH ** -0.5, 0.5, (), jnp.float32),
        "w_right_gate": scatter_about(keys[10], (CH, CH), CH ** -0.5, 0.5, (), jnp.float32),
        "w_out": scatter_about(keys[11], (CH, CH), CH ** -0.5, 0.5, (), jnp.float32),
        "w_out_gate": scatter_about(keys[12], (CH, CH), CH ** -0.5, 0.5, (), jnp.float32),
    }


epsilon = 1e-05

def matmul(left, right):
    return jnp.dot(left, right, precision=lax.Precision.HIGHEST, preferred_element_type=jnp.float32)

def normalize(values):
    center = values - lax.optimization_barrier(jnp.mean(values, axis=-1, keepdims=True))
    inv_std = lax.rsqrt(lax.optimization_barrier(jnp.mean(center * center, axis=-1, keepdims=True)) + epsilon)
    return (center * inv_std, inv_std)

def norm_back(normed, inv_std, upstream):
    mean_up = lax.optimization_barrier(jnp.mean(upstream, axis=-1, keepdims=True))
    mean_proj = lax.optimization_barrier(jnp.mean(upstream * normed, axis=-1, keepdims=True))
    return (upstream - mean_up - normed * mean_proj) * inv_std

def local_front(pair_input, saved_product, pair_grad, pair_mask, w_one, w_two, w_three, w_left, w_left_gate, w_right, w_right_gate, w_out, w_out_gate):
    normed_in, inv_in = normalize(pair_input)
    hidden_one = matmul(normed_in, w_one)
    hidden_two = matmul(normed_in, w_two)
    updated = pair_input + matmul(jax.nn.silu(hidden_one) * hidden_two, w_three)
    normed_mid, inv_mid = normalize(updated)
    left_proj = matmul(normed_mid, w_left)
    left_gate = jax.nn.sigmoid(matmul(normed_mid, w_left_gate))
    right_proj = matmul(normed_mid, w_right)
    right_gate = jax.nn.sigmoid(matmul(normed_mid, w_right_gate))
    left_op = (pair_mask * left_gate * left_proj).astype(jnp.bfloat16)
    right_op = (pair_mask * right_gate * right_proj).astype(jnp.bfloat16)
    normed_out, inv_out = normalize(saved_product)
    out_gate = jax.nn.sigmoid(matmul(normed_mid, w_out_gate))
    gate_term = pair_grad * matmul(normed_out, w_out) * out_gate * (1.0 - out_gate)
    grad_normed = matmul(pair_grad * out_gate, w_out.T)
    grad_product = norm_back(normed_out, inv_out, grad_normed).astype(jnp.bfloat16)
    kept_values = (normed_in, inv_in, hidden_one, hidden_two, normed_mid, inv_mid, left_proj, left_gate, right_proj, right_gate, gate_term)
    return (grad_product, left_op, right_op, kept_values)

def local_back(pair_grad, pair_mask, kept_values, grad_left, grad_right, w_one, w_two, w_three, w_left, w_left_gate, w_right, w_right_gate, w_out_gate):
    normed_in, inv_in, hidden_one, hidden_two, normed_mid, inv_mid, left_proj, left_gate, right_proj, right_gate, gate_term = kept_values
    left_scaled = grad_left * pair_mask * left_gate
    right_scaled = grad_right * pair_mask * right_gate
    grad_mid = matmul(gate_term, w_out_gate.T)
    grad_mid = grad_mid + matmul(left_scaled, w_left.T) + matmul(left_scaled * left_proj * (1.0 - left_gate), w_left_gate.T)
    grad_mid = grad_mid + matmul(right_scaled, w_right.T) + matmul(right_scaled * right_proj * (1.0 - right_gate), w_right_gate.T)
    grad_updated = pair_grad + norm_back(normed_mid, inv_mid, grad_mid)
    grad_hidden = matmul(grad_updated, w_three.T)
    sig_one = jax.nn.sigmoid(hidden_one)
    grad_one = grad_hidden * hidden_two * sig_one * (1.0 + hidden_one * (1.0 - sig_one))
    grad_two = grad_hidden * hidden_one * sig_one
    grad_normed_in = matmul(grad_one, w_one.T) + matmul(grad_two, w_two.T)
    return grad_updated + norm_back(normed_in, inv_in, grad_normed_in)

def reference(pair_input, saved_product, pair_grad, token_mask, w_one, w_two, w_three, w_left, w_left_gate, w_right, w_right_gate, w_out, w_out_gate):
    mask_float = token_mask.astype(jnp.float32)
    pair_mask = (mask_float[:, None] * mask_float[None, :])[:, :, None]
    grad_product, left_op, right_op, kept_values = local_front(pair_input, saved_product, pair_grad, pair_mask, w_one, w_two, w_three, w_left, w_left_gate, w_right, w_right_gate, w_out, w_out_gate)
    product_wide = grad_product.astype(jnp.float32)
    grad_left = jnp.einsum('ijc,jkc->ikc', product_wide, right_op.astype(jnp.float32), precision=lax.Precision.HIGHEST)
    grad_right = jnp.einsum('ijc,ikc->jkc', product_wide, left_op.astype(jnp.float32), precision=lax.Precision.HIGHEST)
    return local_back(pair_grad, pair_mask, kept_values, grad_left, grad_right, w_one, w_two, w_three, w_left, w_left_gate, w_right, w_right_gate, w_out_gate)
```

```python
import functools

import jax
import jax.numpy as jnp
from jax import lax
from jax.experimental import pallas as pl
from jax.experimental.pallas import tpu as pltpu
from jax.sharding import PartitionSpec as P

epsilon = 1e-05
f32 = jnp.float32
bf16 = jnp.bfloat16
MESH = pl.DeviceIdType.MESH


def split(values):
    high = values.astype(bf16)
    return high, (values - high.astype(f32)).astype(bf16)


def dot(values, weights, transposed=False):
    dims = (((1,), (1 if transposed else 0,)), ((), ()))
    return lax.dot_general(values, weights, dimension_numbers=dims, preferred_element_type=f32)


def fold_halves(values):
    half = values.shape[1] // 2
    return values[:, :half] + values[:, half:]


def both_parts(values):
    return jnp.concatenate(split(values), axis=1)


def sigmoid(values):
    return 0.5 * jnp.tanh(0.5 * values) + 0.5


def normalize(values):
    center = values - jnp.mean(values, axis=-1, keepdims=True)
    inv_std = lax.rsqrt(jnp.mean(center * center, axis=-1, keepdims=True) + epsilon)
    return (center * inv_std, inv_std)


def norm_back(normed, inv_std, upstream):
    mean_up = jnp.mean(upstream, axis=-1, keepdims=True)
    mean_proj = jnp.mean(upstream * normed, axis=-1, keepdims=True)
    return (upstream - mean_up - normed * mean_proj) * inv_std


def kernel(
    sizes,
    x_in,
    s_in,
    g_in,
    mask_in,
    w1_in,
    w2_in,
    w3_in,
    wl_in,
    wlg_in,
    wr_in,
    wrg_in,
    wo_in,
    wog_in,
    out_ref,
    w12x,
    w3x,
    w5x,
    w4x,
    wogx,
    wox,
    h1s,
    h2s,
    nms,
    ims,
    nos,
    lgm,
    lq,
    rgm,
    rq,
    gts,
    masks,
    right32,
    accl,
    accr,
    gp32,
    gpt32,
    left_all,
    nm_all,
    gp_row,
    gpt,
    nm_send,
    nm_recv,
    fw_send,
    gx_send,
    gc_send,
    gp_recv,
    gt_send,
    gt_recv,
    gtf_send,
    in_sem,
    x_ref,
    s_ref,
    g_ref,
    mask_ref,
    w1_ref,
    w2_ref,
    w3_ref,
    wl_ref,
    wlg_ref,
    wr_ref,
    wrg_ref,
    wo_ref,
    wog_ref,
):
    rows, pairs, tr, tc, tokens, n_col, n_ch, chunk, ktile = sizes
    n_z = rows // 2
    ratio = tc // tr
    width = out_ref.shape[1]
    hid = w1_in.shape[1]
    steps = pairs // chunk
    row = lax.axis_index("row")
    my_z, my_y = row // 2, row % 2
    col, ch = lax.axis_index("col"), lax.axis_index("ch")
    my_k = col * n_ch + ch
    y_peer = my_z * 2 + (1 - my_y)

    def z_valid(delta):
        return (my_z + delta >= 0) & (my_z + delta < n_z)

    def z_row(delta):
        return (my_z + delta) * 2 + my_y

    def col_at(dcol):
        return lax.rem(col + dcol, n_col)

    def ch_at(dch):
        return lax.rem(ch + dch, n_ch)

    barrier = pltpu.get_barrier_semaphore()
    for far in range(1, rows):
        pl.semaphore_signal(barrier, inc=1, device_id={"row": lax.rem(row + far, rows)}, device_id_type=MESH)
    for dcol in range(1, n_col):
        pl.semaphore_signal(barrier, inc=1, device_id={"col": col_at(dcol)}, device_id_type=MESH)
    for dch in range(1, n_ch):
        pl.semaphore_signal(barrier, inc=1, device_id={"ch": ch_at(dch)}, device_id_type=MESH)

    inputs = []
    for source, target in (
        (x_in, x_ref),
        (w1_in, w1_ref),
        (w2_in, w2_ref),
        (mask_in, mask_ref),
        (w3_in, w3_ref),
        (wog_in, wog_ref),
        (wo_in, wo_ref),
        (s_in, s_ref),
        (g_in, g_ref),
        (wl_in, wl_ref),
        (wlg_in, wlg_ref),
        (wr_in, wr_ref),
        (wrg_in, wrg_ref),
    ):
        copy = pltpu.make_async_copy(source, target, in_sem.at[len(inputs)])
        copy.start()
        inputs.append(copy)

    def loaded(count):
        for _ in range(count):
            inputs.pop(0).wait()

    def put(source, high_at, low_at):
        high, low = split(source[...])
        for ref, at in high_at:
            ref[at[0] : at[0] + high.shape[0], at[1] : at[1] + high.shape[1]] = high
        ref, at = low_at
        ref[at[0] : at[0] + high.shape[0], at[1] : at[1] + high.shape[1]] = low

    def put_tall(target, source, at):
        put(source, [(target, (0, at)), (target, (width, at))], (target, (2 * width, at)))

    loaded(5)
    put_tall(w12x, w1_ref, 0)
    put_tall(w12x, w2_ref, hid)
    put(w3_ref, [(w3x, (0, 0)), (w3x, (0, width))], (w3x, (0, 2 * width)))

    token = lax.broadcasted_iota(jnp.int32, (tc, tokens), 1)
    spot = lax.broadcasted_iota(jnp.int32, (tc, tokens), 0)
    mask = mask_ref[...].astype(f32)
    col_mask = jnp.sum(
        jnp.where(token == spot + my_k * tc, jnp.broadcast_to(mask, (tc, tokens)), 0.0), axis=1, keepdims=True
    )
    col_mask = jnp.concatenate([jnp.broadcast_to(col_mask, (tc, 128))] * (chunk // tc), axis=0)

    def front(step, carry):
        base = pl.multiple_of(step * chunk, chunk)
        here = pl.ds(base, chunk)
        token = lax.broadcasted_iota(jnp.int32, (chunk, tokens), 1)
        spot = lax.broadcasted_iota(jnp.int32, (chunk, tokens), 0) + base
        ahead = spot - (token - row * tr) * tc
        row_mask = jnp.sum(
            jnp.where((ahead >= 0) & (ahead < tc), jnp.broadcast_to(mask, (chunk, tokens)), 0.0), axis=1, keepdims=True
        )
        masks[here, :] = col_mask * row_mask
        pair_input = x_ref[here, :]
        normed_in, _ = normalize(pair_input)
        parts = both_parts(normed_in)
        hidden = dot(parts, w12x[: 2 * width, :]) + dot(parts[:, :width], w12x[2 * width :, :])
        hidden_one, hidden_two = hidden[:, :hid], hidden[:, hid:]
        h1s[here, :] = hidden_one
        h2s[here, :] = hidden_two
        act = hidden_one * sigmoid(hidden_one) * hidden_two
        high, low = split(act)
        updated = pair_input + (fold_halves(dot(high, w3x[:, width:])) + dot(low, w3x[:, :width]))
        normed_mid, inv_mid = normalize(updated)
        nms[here, :] = normed_mid
        ims[here, :] = jnp.broadcast_to(inv_mid, (chunk, 128))
        nm_all[row, here, :] = normed_mid.astype(bf16)
        return carry

    lax.fori_loop(0, steps, front, 0)
    pl.semaphore_wait(barrier, rows - 1 + n_col - 1 + n_ch - 1)

    def nm_copy(slot, sem, target):
        return pltpu.make_async_remote_copy(
            src_ref=nm_all.at[slot],
            dst_ref=nm_all.at[slot],
            send_sem=sem,
            recv_sem=nm_recv.at[slot],
            device_id={"row": target},
            device_id_type=MESH,
        )

    sends = []
    held = []

    def start(copy):
        copy.start()
        sends.append(copy)

    def start_if(cond, copy):
        pl.when(cond)(copy.start)
        held.append((cond, copy))

    def slot_copy(slot, sem, target):
        place = gp_row.at[pl.ds(slot * ratio, ratio)]
        return pltpu.make_async_remote_copy(
            src_ref=place,
            dst_ref=place,
            send_sem=sem,
            recv_sem=gp_recv.at[slot],
            device_id=target,
            device_id_type=MESH,
        )

    def piece_copy(target_row):
        return pltpu.make_async_remote_copy(
            src_ref=gp_row.at[target_row],
            dst_ref=gpt.at[row],
            send_sem=gt_send.at[target_row],
            recv_sem=gt_recv.at[row],
            device_id={"row": target_row},
            device_id_type=MESH,
        )

    def share_copy(source_row, dch):
        return pltpu.make_async_remote_copy(
            src_ref=gpt.at[source_row],
            dst_ref=gpt.at[source_row],
            send_sem=gtf_send.at[dch - 1, source_row],
            recv_sem=gt_recv.at[source_row],
            device_id={"ch": ch_at(dch)},
            device_id_type=MESH,
        )

    for far in range(1, n_z):
        for delta in (far, -far):
            sem = nm_send.at[2 * far - 1 + (delta < 0)]
            start_if(z_valid(delta), nm_copy(row, sem, z_row(delta)))
    start(nm_copy(row, nm_send.at[0], y_peer))

    loaded(4)
    put(wog_ref, [(wogx, (0, 0)), (wogx, (width, 0))], (wogx, (0, width)))
    put(wo_ref, [(wox, (0, 0)), (wox, (0, width))], (wox, (width, 0)))
    wogx[width:, width:] = jnp.zeros((width, width), bf16)
    wox[width:, width:] = jnp.zeros((width, width), bf16)

    for step in range(steps):
        here = pl.ds(step * chunk, chunk)
        out_gate = sigmoid(fold_halves(dot(both_parts(nms[here, :]), wogx[...])))
        pair_grad = g_ref[here, :]
        normed_out, inv_out = normalize(s_ref[here, :])
        nos[here, :] = normed_out.astype(bf16)
        grad_normed = fold_halves(dot(both_parts(pair_grad * out_gate), wox[...], True))
        product = norm_back(normed_out, inv_out, grad_normed).astype(bf16).astype(f32) * masks[here, :]
        gts[here, :] = pair_grad * out_gate * (1.0 - out_gate)
        for i in range(chunk // tc):
            for part in range(ratio):
                at = (step * (chunk // tc) + i) * tr
                gp32[my_k * ratio + part, at : at + tr, :] = product[i * tc + part * tr : i * tc + (part + 1) * tr, :]

    for part in range(ratio):
        gp_row[my_k * ratio + part] = gp32[my_k * ratio + part].astype(bf16)

    def pieces(dcol):
        for part in range(ratio):
            target_row = (col_at(dcol) * n_ch + ch) * ratio + part
            start_if(target_row != row, piece_copy(target_row))

    def gather_share(dcol):
        slot = col_at(dcol) * n_ch + ch
        for dch in range(1, n_ch):
            start(slot_copy(slot, gc_send.at[dch - 1, slot], {"ch": ch_at(dch)}))

    for dcol in range(1, n_col):
        start(slot_copy(my_k, gx_send.at[dcol], {"col": col_at(dcol)}))
    gather_share(0)
    pieces(0)

    loaded(4)
    put_tall(w5x, wl_ref, 0)
    put_tall(w5x, wlg_ref, width)
    put_tall(w5x, wr_ref, 2 * width)
    put_tall(w5x, wrg_ref, 3 * width)
    w4x[...] = w5x[width:, :] * bf16(0.5)

    def own(step, carry):
        here = pl.ds(pl.multiple_of(step * chunk, chunk), chunk)
        parts = both_parts(nms[here, :])
        proj = dot(parts, w5x[: 2 * width, :]) + dot(parts[:, :width], w5x[2 * width :, :])
        left_proj, left_gate = proj[:, :128], sigmoid(proj[:, 128:256])
        right_proj, right_gate = proj[:, 256:384], sigmoid(proj[:, 384:])
        pair_mask = masks[here, :]
        lgm[here, :] = pair_mask * left_gate
        lq[here, :] = left_proj * (1.0 - left_gate)
        rgm[here, :] = pair_mask * right_gate
        rq[here, :] = right_proj * (1.0 - right_gate)
        left_all[row, here, :] = (left_gate * left_proj).astype(bf16).astype(f32)
        right32[here, :] = (right_gate * right_proj).astype(bf16).astype(f32)
        return carry

    lax.fori_loop(0, steps, own, 0)

    def middle(step, carry):
        here = pl.ds(pl.multiple_of(step * 48, 48), 48)
        hidden_one, hidden_two = h1s[here, :], h2s[here, :]
        sig_one = sigmoid(hidden_one)
        h1s[here, :] = hidden_two * sig_one * (1.0 + hidden_one * (1.0 - sig_one))
        h2s[here, :] = hidden_one * sig_one
        return carry

    def gate_back(step, carry):
        here = pl.ds(pl.multiple_of(step * chunk, chunk), chunk)
        gate_term = gts[here, :] * dot(nos[here, :], wox[:width, :width])
        gts[here, :] = dot(gate_term.astype(bf16), wogx[:width, :width], True)
        return carry

    def widen(slot):
        for part in range(ratio):
            gp32[slot * ratio + part] = gp_row[slot * ratio + part].astype(f32)

    k_bases = range(0, tc, ktile)

    def fold_left(owner, first):
        for k_base in k_bases:

            def body(j, acc):
                tile = right32[pl.ds(pl.multiple_of(j * tc + k_base, 8), ktile), :]
                return tuple(acc[i] + gp32[owner, pl.ds(i * tr + j, 1), :] * tile for i in range(tr))

            begin = tuple(
                jnp.zeros((ktile, 128), f32) if first else accl[pl.ds(i * tc + k_base, ktile), :] for i in range(tr)
            )
            acc = lax.fori_loop(0, tr, body, begin, unroll=True)
            for i in range(tr):
                accl[pl.ds(i * tc + k_base, ktile), :] = acc[i]

    def fold_right(source, first):
        if first:
            gpt32[...] = gp32[row]
        else:
            gpt32[...] = gpt[source].astype(f32)
        for k_base in k_bases:

            def body(i, acc):
                tile = left_all[source, pl.ds(pl.multiple_of(i * tc + k_base, 8), ktile), :]
                return tuple(acc[j] + gpt32[pl.ds(i * tr + j, 1), :] * tile for j in range(tr))

            begin = tuple(
                jnp.zeros((ktile, 128), f32) if first else accr[pl.ds(j * tc + k_base, ktile), :] for j in range(tr)
            )
            acc = lax.fori_loop(0, tr, body, begin, unroll=True)
            for j in range(tr):
                accr[pl.ds(j * tc + k_base, ktile), :] = acc[j]

    def block(source):
        def project(step, carry):
            here = pl.ds(pl.multiple_of(step * chunk, chunk), chunk)
            values = nm_all[source, here, :]
            proj = dot(jnp.concatenate([values, values], axis=1), w4x[...])
            left_half, right_half = proj[:, :128], proj[:, 256:384]
            left_all[source, here, :] = left_half * jnp.tanh(proj[:, 128:256]) + left_half
            right32[here, :] = right_half * jnp.tanh(proj[:, 384:]) + right_half
            return carry

        lax.fori_loop(0, steps, project, 0)
        fold_left(source, False)

    lax.fori_loop(0, pairs // 48, middle, 0)
    lax.fori_loop(0, steps, gate_back, 0)

    for dcol in range(1, n_col):
        slot = col_at(dcol) * n_ch + ch
        slot_copy(slot, gx_send.at[dcol], {"col": col_at(dcol)}).wait_recv()
        gather_share(dcol)
        pieces(dcol)
        widen(slot)
    for dcol in range(n_col):
        for dch in range(1, n_ch):
            slot = col_at(dcol) * n_ch + ch_at(dch)
            slot_copy(slot, gc_send.at[dch - 1, slot], {"ch": ch_at(dch)}).wait_recv()
            widen(slot)
    fold_left(row, True)
    fold_right(row, True)

    def delta_of(index):
        return (index // 2 + 1) * (1 - 2 * lax.rem(index, 2))

    def z_block(index, carry):
        delta = delta_of(index)

        @pl.when(z_valid(delta))
        def _():
            source = z_row(delta)
            forward = nm_copy(source, fw_send.at[index], y_peer)
            forward.wait_recv()
            forward.start()
            block(source)

        return carry

    def y_block(source):
        nm_copy(source, fw_send.at[0], y_peer).wait_recv()
        block(source)

    def y_blocks(index, carry):
        delta = delta_of(index)

        @pl.when(z_valid(delta))
        def _():
            y_block((my_z + delta) * 2 + (1 - my_y))

        return carry

    y_block(y_peer)
    lax.fori_loop(0, 2 * n_z - 2, z_block, 0)

    head = lax.rem(row // ratio, n_ch) == ch

    def share(far, carry):
        source = lax.rem(row + far, rows)
        share_copy(source, 1).wait_recv()

        @pl.when(head)
        def _():
            for dch in range(1, n_ch):
                share_copy(source, dch).start()

        return carry

    lax.fori_loop(1, rows, share, 0)
    lax.fori_loop(0, 2 * n_z - 2, y_blocks, 0)

    def rights(far, carry):
        fold_right(lax.rem(row + far, rows), False)
        return carry

    lax.fori_loop(1, rows, rights, 0)

    def back(step, carry):
        here = pl.ds(pl.multiple_of(step * chunk, chunk), chunk)
        left_scaled = accl[here, :] * lgm[here, :]
        right_scaled = accr[here, :] * rgm[here, :]
        wide = jnp.concatenate(
            [left_scaled, left_scaled * lq[here, :], right_scaled, right_scaled * rq[here, :]], axis=1
        )
        high, low = split(wide)
        grad_mid = gts[here, :] + (fold_halves(dot(high, w5x[width:, :], True)) + dot(low, w5x[:width, :], True))
        grad_updated = g_ref[here, :] + norm_back(nms[here, :], ims[here, :], grad_mid)
        grad_hidden = dot(both_parts(grad_updated), w3x[:, : 2 * width], True)
        both = jnp.concatenate([grad_hidden * h1s[here, :], grad_hidden * h2s[here, :]], axis=1)
        grad_normed_in = fold_halves(dot(both.astype(bf16), w12x[width:, :], True))
        normed_in, inv_in = normalize(x_ref[here, :])
        out_ref[here, :] = grad_updated + norm_back(normed_in, inv_in, grad_normed_in)
        return carry

    lax.fori_loop(0, steps, back, 0)

    for copy in sends:
        copy.wait_send()
    for cond, copy in held:
        pl.when(cond)(copy.wait_send)

    def forwarded(index, carry):
        delta = delta_of(index)

        @pl.when(z_valid(delta))
        def _():
            nm_copy(z_row(delta), fw_send.at[index], y_peer).wait_send()

        return carry

    lax.fori_loop(0, 2 * n_z - 2, forwarded, 0)

    @pl.when(head)
    def _():
        def shared(far, carry):
            for dch in range(1, n_ch):
                share_copy(lax.rem(row + far, rows), dch).wait_send()
            return carry

        lax.fori_loop(1, rows, shared, 0)


def per_device(mesh, pair_input, saved_product, pair_grad, token_mask, *weights):
    rows = mesh.shape["row"]
    n_col, n_ch = mesh.shape["col"], mesh.shape["ch"]
    tr, tc, width = pair_input.shape
    pairs = tr * tc
    tokens = token_mask.shape[0]
    hid = weights[0].shape[1]
    chunk = 288 if pairs % 288 == 0 else pairs
    ktile = 24 if tc % 24 == 0 else tc
    n_k, n_z = n_col * n_ch, rows // 2
    flat = [array.reshape(pairs, width) for array in (pair_input, saved_product, pair_grad)]
    arrays = [*flat, token_mask.reshape(1, tokens), *weights]
    vmem = pltpu.VMEM
    dma = pltpu.SemaphoreType.DMA
    tile32 = vmem((pairs, width), f32)
    sizes = (rows, pairs, tr, tc, tokens, n_col, n_ch, chunk, ktile)
    out = pl.pallas_call(
        functools.partial(kernel, sizes),
        out_shape=jax.ShapeDtypeStruct((pairs, width), f32),
        in_specs=[pl.BlockSpec(memory_space=pl.ANY)] * 13,
        out_specs=pl.BlockSpec(memory_space=vmem),
        scratch_shapes=[
            vmem((3 * width, 2 * hid), bf16),
            vmem((hid, 3 * width), bf16),
            vmem((3 * width, 4 * width), bf16),
            vmem((2 * width, 4 * width), bf16),
            vmem((2 * width, 2 * width), bf16),
            vmem((2 * width, 2 * width), bf16),
            vmem((pairs, hid), f32),
            vmem((pairs, hid), f32),
            tile32,
            tile32,
            vmem((pairs, width), bf16),
            *([tile32] * 9),
            vmem((rows, tr * tr, width), f32),
            vmem((tr * tr, width), f32),
            vmem((rows, pairs, width), f32),
            vmem((rows, pairs, width), bf16),
            vmem((rows, tr * tr, width), bf16),
            vmem((rows, tr * tr, width), bf16),
            dma((2 * n_z,)),
            dma((rows,)),
            dma((2 * n_z,)),
            dma((n_col,)),
            dma((n_ch, n_k)),
            dma((n_k,)),
            dma((rows,)),
            dma((rows,)),
            dma((n_ch, rows)),
            dma((13,)),
            *[vmem(array.shape, array.dtype) for array in arrays],
        ],
        compiler_params=pltpu.CompilerParams(
            collective_id=0, has_side_effects=True, vmem_limit_bytes=60 * 1024 * 1024
        ),
    )(*arrays)
    return out.reshape(tr, tc, width)


def solution(mesh):
    tile = P(("grp", "row"), ("col", "ch"), None)
    in_specs = (tile, tile, tile, P("grp")) + (P(),) * 9
    return jax.shard_map(
        functools.partial(per_device, mesh), mesh=mesh, in_specs=in_specs, out_specs=tile, check_vma=False
    )
```

```python
import functools

import jax
import jax.numpy as jnp
from jax import lax
from jax.experimental import pallas as pl
from jax.experimental.pallas import tpu as pltpu
from jax.sharding import PartitionSpec as P

epsilon = 1e-05
f32 = jnp.float32
bf16 = jnp.bfloat16
MESH = pl.DeviceIdType.MESH


def split(values):
    high = values.astype(bf16)
    return high, (values - high.astype(f32)).astype(bf16)


def dot(values, weights, transposed=False):
    dims = (((1,), (1 if transposed else 0,)), ((), ()))
    return lax.dot_general(values, weights, dimension_numbers=dims, preferred_element_type=f32)


def fold_halves(values):
    half = values.shape[1] // 2
    return values[:, :half] + values[:, half:]


def both_parts(values):
    return jnp.concatenate(split(values), axis=1)


def sigmoid(values):
    return 0.5 * jnp.tanh(0.5 * values) + 0.5


def normalize(values):
    center = values - jnp.mean(values, axis=-1, keepdims=True)
    inv_std = lax.rsqrt(jnp.mean(center * center, axis=-1, keepdims=True) + epsilon)
    return (center * inv_std, inv_std)


def norm_back(normed, inv_std, upstream):
    mean_up = jnp.mean(upstream, axis=-1, keepdims=True)
    mean_proj = jnp.mean(upstream * normed, axis=-1, keepdims=True)
    return (upstream - mean_up - normed * mean_proj) * inv_std


def kernel(
    sizes,
    x_in,
    s_in,
    g_in,
    mask_in,
    w1_in,
    w2_in,
    w3_in,
    wl_in,
    wlg_in,
    wr_in,
    wrg_in,
    wo_in,
    wog_in,
    out_ref,
    w12x,
    w3x,
    w5x,
    w4x,
    wogx,
    wox,
    h1s,
    h2s,
    nms,
    ims,
    nos,
    lgm,
    lq,
    rgm,
    rq,
    gts,
    masks,
    right32,
    accl,
    accr,
    gp32,
    gpt32,
    left_all,
    nm_all,
    gp_row,
    gpt,
    nm_send,
    nm_recv,
    fw_send,
    gx_send,
    gc_send,
    gp_recv,
    gt_send,
    gt_recv,
    gtf_send,
    in_sem,
    x_ref,
    s_ref,
    g_ref,
    mask_ref,
    w1_ref,
    w2_ref,
    w3_ref,
    wl_ref,
    wlg_ref,
    wr_ref,
    wrg_ref,
    wo_ref,
    wog_ref,
):
    rows, pairs, tr, tc, tokens, n_col, n_ch, chunk, ktile = sizes
    n_z = rows // 2
    ratio = tc // tr
    width = out_ref.shape[1]
    hid = w1_in.shape[1]
    steps = pairs // chunk
    row = lax.axis_index("row")
    my_z, my_y = row // 2, row % 2
    col, ch = lax.axis_index("col"), lax.axis_index("ch")
    my_k = col * n_ch + ch
    y_peer = my_z * 2 + (1 - my_y)

    def z_valid(delta):
        return (my_z + delta >= 0) & (my_z + delta < n_z)

    def z_row(delta):
        return (my_z + delta) * 2 + my_y

    def col_at(dcol):
        return lax.rem(col + dcol, n_col)

    def ch_at(dch):
        return lax.rem(ch + dch, n_ch)

    barrier = pltpu.get_barrier_semaphore()
    for far in range(1, rows):
        pl.semaphore_signal(barrier, inc=1, device_id={"row": lax.rem(row + far, rows)}, device_id_type=MESH)
    for dcol in range(1, n_col):
        pl.semaphore_signal(barrier, inc=1, device_id={"col": col_at(dcol)}, device_id_type=MESH)
    for dch in range(1, n_ch):
        pl.semaphore_signal(barrier, inc=1, device_id={"ch": ch_at(dch)}, device_id_type=MESH)

    inputs = []
    for source, target in (
        (x_in, x_ref),
        (w1_in, w1_ref),
        (w2_in, w2_ref),
        (mask_in, mask_ref),
        (w3_in, w3_ref),
        (wog_in, wog_ref),
        (wo_in, wo_ref),
        (s_in, s_ref),
        (g_in, g_ref),
        (wl_in, wl_ref),
        (wlg_in, wlg_ref),
        (wr_in, wr_ref),
        (wrg_in, wrg_ref),
    ):
        copy = pltpu.make_async_copy(source, target, in_sem.at[len(inputs)])
        copy.start()
        inputs.append(copy)

    def loaded(count):
        for _ in range(count):
            inputs.pop(0).wait()

    def put(source, high_at, low_at):
        high, low = split(source[...])
        for ref, at in high_at:
            ref[at[0] : at[0] + high.shape[0], at[1] : at[1] + high.shape[1]] = high
        ref, at = low_at
        ref[at[0] : at[0] + high.shape[0], at[1] : at[1] + high.shape[1]] = low

    def put_tall(target, source, at):
        put(source, [(target, (0, at)), (target, (width, at))], (target, (2 * width, at)))

    loaded(5)
    put_tall(w12x, w1_ref, 0)
    put_tall(w12x, w2_ref, hid)
    put(w3_ref, [(w3x, (0, 0)), (w3x, (0, width))], (w3x, (0, 2 * width)))

    token = lax.broadcasted_iota(jnp.int32, (tc, tokens), 1)
    spot = lax.broadcasted_iota(jnp.int32, (tc, tokens), 0)
    mask = mask_ref[...].astype(f32)
    col_mask = jnp.sum(
        jnp.where(token == spot + my_k * tc, jnp.broadcast_to(mask, (tc, tokens)), 0.0), axis=1, keepdims=True
    )
    col_mask = jnp.concatenate([jnp.broadcast_to(col_mask, (tc, 128))] * (chunk // tc), axis=0)

    def front(step, carry):
        base = pl.multiple_of(step * chunk, chunk)
        here = pl.ds(base, chunk)
        token = lax.broadcasted_iota(jnp.int32, (chunk, tokens), 1)
        spot = lax.broadcasted_iota(jnp.int32, (chunk, tokens), 0) + base
        ahead = spot - (token - row * tr) * tc
        row_mask = jnp.sum(
            jnp.where((ahead >= 0) & (ahead < tc), jnp.broadcast_to(mask, (chunk, tokens)), 0.0), axis=1, keepdims=True
        )
        masks[here, :] = col_mask * row_mask
        pair_input = x_ref[here, :]
        normed_in, _ = normalize(pair_input)
        parts = both_parts(normed_in)
        hidden = dot(parts, w12x[: 2 * width, :]) + dot(parts[:, :width], w12x[2 * width :, :])
        hidden_one, hidden_two = hidden[:, :hid], hidden[:, hid:]
        h1s[here, :] = hidden_one
        h2s[here, :] = hidden_two
        act = hidden_one * sigmoid(hidden_one) * hidden_two
        high, low = split(act)
        updated = pair_input + (fold_halves(dot(high, w3x[:, width:])) + dot(low, w3x[:, :width]))
        normed_mid, inv_mid = normalize(updated)
        nms[here, :] = normed_mid
        ims[here, :] = jnp.broadcast_to(inv_mid, (chunk, 128))
        nm_all[row, here, :] = normed_mid.astype(bf16)
        return carry

    lax.fori_loop(0, steps, front, 0)
    pl.semaphore_wait(barrier, rows - 1 + n_col - 1 + n_ch - 1)

    def nm_copy(slot, sem, target):
        return pltpu.make_async_remote_copy(
            src_ref=nm_all.at[slot],
            dst_ref=nm_all.at[slot],
            send_sem=sem,
            recv_sem=nm_recv.at[slot],
            device_id={"row": target},
            device_id_type=MESH,
        )

    sends = []
    held = []

    def start(copy):
        copy.start()
        sends.append(copy)

    def start_if(cond, copy):
        pl.when(cond)(copy.start)
        held.append((cond, copy))

    def slot_copy(slot, sem, target):
        place = gp_row.at[pl.ds(slot * ratio, ratio)]
        return pltpu.make_async_remote_copy(
            src_ref=place,
            dst_ref=place,
            send_sem=sem,
            recv_sem=gp_recv.at[slot],
            device_id=target,
            device_id_type=MESH,
        )

    def piece_copy(target_row):
        return pltpu.make_async_remote_copy(
            src_ref=gp_row.at[target_row],
            dst_ref=gpt.at[row],
            send_sem=gt_send.at[target_row],
            recv_sem=gt_recv.at[row],
            device_id={"row": target_row},
            device_id_type=MESH,
        )

    def share_copy(source_row, dch):
        return pltpu.make_async_remote_copy(
            src_ref=gpt.at[source_row],
            dst_ref=gpt.at[source_row],
            send_sem=gtf_send.at[dch - 1, source_row],
            recv_sem=gt_recv.at[source_row],
            device_id={"ch": ch_at(dch)},
            device_id_type=MESH,
        )

    for far in range(n_z - 1, 0, -1):
        for delta in (far, -far):
            sem = nm_send.at[2 * far - 1 + (delta < 0)]
            start_if(z_valid(delta), nm_copy(row, sem, z_row(delta)))
    start(nm_copy(row, nm_send.at[0], y_peer))

    loaded(4)
    put(wog_ref, [(wogx, (0, 0)), (wogx, (width, 0))], (wogx, (0, width)))
    put(wo_ref, [(wox, (0, 0)), (wox, (0, width))], (wox, (width, 0)))
    wogx[width:, width:] = jnp.zeros((width, width), bf16)
    wox[width:, width:] = jnp.zeros((width, width), bf16)

    for step in range(steps):
        here = pl.ds(step * chunk, chunk)
        out_gate = sigmoid(fold_halves(dot(both_parts(nms[here, :]), wogx[...])))
        pair_grad = g_ref[here, :]
        normed_out, inv_out = normalize(s_ref[here, :])
        nos[here, :] = normed_out.astype(bf16)
        grad_normed = fold_halves(dot(both_parts(pair_grad * out_gate), wox[...], True))
        product = norm_back(normed_out, inv_out, grad_normed).astype(bf16).astype(f32) * masks[here, :]
        gts[here, :] = pair_grad * out_gate * (1.0 - out_gate)
        for i in range(chunk // tc):
            for part in range(ratio):
                at = (step * (chunk // tc) + i) * tr
                gp32[my_k * ratio + part, at : at + tr, :] = product[i * tc + part * tr : i * tc + (part + 1) * tr, :]

    for part in range(ratio):
        gp_row[my_k * ratio + part] = gp32[my_k * ratio + part].astype(bf16)

    def pieces(dcol):
        for part in range(ratio):
            target_row = (col_at(dcol) * n_ch + ch) * ratio + part
            start_if(target_row != row, piece_copy(target_row))

    def gather_share(dcol):
        slot = col_at(dcol) * n_ch + ch
        for dch in range(1, n_ch):
            start(slot_copy(slot, gc_send.at[dch - 1, slot], {"ch": ch_at(dch)}))

    for dcol in range(1, n_col):
        start(slot_copy(my_k, gx_send.at[dcol], {"col": col_at(dcol)}))
    gather_share(0)
    pieces(0)

    loaded(4)
    put_tall(w5x, wl_ref, 0)
    put_tall(w5x, wlg_ref, width)
    put_tall(w5x, wr_ref, 2 * width)
    put_tall(w5x, wrg_ref, 3 * width)
    w4x[...] = w5x[width:, :] * bf16(0.5)

    def own(step, carry):
        here = pl.ds(pl.multiple_of(step * chunk, chunk), chunk)
        parts = both_parts(nms[here, :])
        proj = dot(parts, w5x[: 2 * width, :]) + dot(parts[:, :width], w5x[2 * width :, :])
        left_proj, left_gate = proj[:, :128], sigmoid(proj[:, 128:256])
        right_proj, right_gate = proj[:, 256:384], sigmoid(proj[:, 384:])
        pair_mask = masks[here, :]
        lgm[here, :] = pair_mask * left_gate
        lq[here, :] = left_proj * (1.0 - left_gate)
        rgm[here, :] = pair_mask * right_gate
        rq[here, :] = right_proj * (1.0 - right_gate)
        left_all[row, here, :] = (left_gate * left_proj).astype(bf16).astype(f32)
        right32[here, :] = (right_gate * right_proj).astype(bf16).astype(f32)
        return carry

    lax.fori_loop(0, steps, own, 0)

    def middle(step, carry):
        here = pl.ds(pl.multiple_of(step * 48, 48), 48)
        hidden_one, hidden_two = h1s[here, :], h2s[here, :]
        sig_one = sigmoid(hidden_one)
        h1s[here, :] = hidden_two * sig_one * (1.0 + hidden_one * (1.0 - sig_one))
        h2s[here, :] = hidden_one * sig_one
        return carry

    def gate_back(step, carry):
        here = pl.ds(pl.multiple_of(step * chunk, chunk), chunk)
        gate_term = gts[here, :] * dot(nos[here, :], wox[:width, :width])
        gts[here, :] = dot(gate_term.astype(bf16), wogx[:width, :width], True)
        return carry

    def widen(slot):
        for part in range(ratio):
            gp32[slot * ratio + part] = gp_row[slot * ratio + part].astype(f32)

    k_bases = range(0, tc, ktile)

    def fold_left(owner, first):
        for k_base in k_bases:

            def body(j, acc):
                tile = right32[pl.ds(pl.multiple_of(j * tc + k_base, 8), ktile), :]
                return tuple(acc[i] + gp32[owner, pl.ds(i * tr + j, 1), :] * tile for i in range(tr))

            begin = tuple(
                jnp.zeros((ktile, 128), f32) if first else accl[pl.ds(i * tc + k_base, ktile), :] for i in range(tr)
            )
            acc = lax.fori_loop(0, tr, body, begin, unroll=True)
            for i in range(tr):
                accl[pl.ds(i * tc + k_base, ktile), :] = acc[i]

    def fold_right(source, first):
        if first:
            gpt32[...] = gp32[row]
        else:
            gpt32[...] = gpt[source].astype(f32)
        for k_base in k_bases:

            def body(i, acc):
                tile = left_all[source, pl.ds(pl.multiple_of(i * tc + k_base, 8), ktile), :]
                return tuple(acc[j] + gpt32[pl.ds(i * tr + j, 1), :] * tile for j in range(tr))

            begin = tuple(
                jnp.zeros((ktile, 128), f32) if first else accr[pl.ds(j * tc + k_base, ktile), :] for j in range(tr)
            )
            acc = lax.fori_loop(0, tr, body, begin, unroll=True)
            for j in range(tr):
                accr[pl.ds(j * tc + k_base, ktile), :] = acc[j]

    def block(source):
        def project(step, carry):
            here = pl.ds(pl.multiple_of(step * chunk, chunk), chunk)
            values = nm_all[source, here, :]
            proj = dot(jnp.concatenate([values, values], axis=1), w4x[...])
            left_half, right_half = proj[:, :128], proj[:, 256:384]
            left_all[source, here, :] = left_half * jnp.tanh(proj[:, 128:256]) + left_half
            right32[here, :] = right_half * jnp.tanh(proj[:, 384:]) + right_half
            return carry

        lax.fori_loop(0, steps, project, 0)
        fold_left(source, False)

    lax.fori_loop(0, pairs // 48, middle, 0)
    lax.fori_loop(0, steps, gate_back, 0)

    for dcol in range(1, n_col):
        slot = col_at(dcol) * n_ch + ch
        slot_copy(slot, gx_send.at[dcol], {"col": col_at(dcol)}).wait_recv()
        gather_share(dcol)
        pieces(dcol)
        widen(slot)
    for dcol in range(n_col):
        for dch in range(1, n_ch):
            slot = col_at(dcol) * n_ch + ch_at(dch)
            slot_copy(slot, gc_send.at[dch - 1, slot], {"ch": ch_at(dch)}).wait_recv()
            widen(slot)
    fold_left(row, True)
    fold_right(row, True)

    def delta_of(index):
        return (index // 2 + 1) * (1 - 2 * lax.rem(index, 2))

    def z_block(index, carry):
        delta = delta_of(index)

        @pl.when(z_valid(delta))
        def _():
            source = z_row(delta)
            forward = nm_copy(source, fw_send.at[index], y_peer)
            forward.wait_recv()
            forward.start()
            block(source)

        return carry

    def y_block(source):
        nm_copy(source, fw_send.at[0], y_peer).wait_recv()
        block(source)

    def y_blocks(index, carry):
        delta = delta_of(index)

        @pl.when(z_valid(delta))
        def _():
            y_block((my_z + delta) * 2 + (1 - my_y))

        return carry

    y_block(y_peer)
    lax.fori_loop(0, 2 * n_z - 2, z_block, 0)

    head = lax.rem(row // ratio, n_ch) == ch

    def share(far, carry):
        source = lax.rem(row + far, rows)
        share_copy(source, 1).wait_recv()

        @pl.when(head)
        def _():
            for dch in range(1, n_ch):
                share_copy(source, dch).start()

        return carry

    lax.fori_loop(1, rows, share, 0)
    lax.fori_loop(0, 2 * n_z - 2, y_blocks, 0)

    def rights(far, carry):
        fold_right(lax.rem(row + far, rows), False)
        return carry

    lax.fori_loop(1, rows, rights, 0)

    def back(step, carry):
        here = pl.ds(pl.multiple_of(step * chunk, chunk), chunk)
        left_scaled = accl[here, :] * lgm[here, :]
        right_scaled = accr[here, :] * rgm[here, :]
        wide = jnp.concatenate(
            [left_scaled, left_scaled * lq[here, :], right_scaled, right_scaled * rq[here, :]], axis=1
        )
        high, low = split(wide)
        grad_mid = gts[here, :] + (fold_halves(dot(high, w5x[width:, :], True)) + dot(low, w5x[:width, :], True))
        grad_updated = g_ref[here, :] + norm_back(nms[here, :], ims[here, :], grad_mid)
        grad_hidden = dot(both_parts(grad_updated), w3x[:, : 2 * width], True)
        both = jnp.concatenate([grad_hidden * h1s[here, :], grad_hidden * h2s[here, :]], axis=1)
        grad_normed_in = fold_halves(dot(both.astype(bf16), w12x[width:, :], True))
        normed_in, inv_in = normalize(x_ref[here, :])
        out_ref[here, :] = grad_updated + norm_back(normed_in, inv_in, grad_normed_in)
        return carry

    lax.fori_loop(0, steps, back, 0)

    for copy in sends:
        copy.wait_send()
    for cond, copy in held:
        pl.when(cond)(copy.wait_send)

    def forwarded(index, carry):
        delta = delta_of(index)

        @pl.when(z_valid(delta))
        def _():
            nm_copy(z_row(delta), fw_send.at[index], y_peer).wait_send()

        return carry

    lax.fori_loop(0, 2 * n_z - 2, forwarded, 0)

    @pl.when(head)
    def _():
        def shared(far, carry):
            for dch in range(1, n_ch):
                share_copy(lax.rem(row + far, rows), dch).wait_send()
            return carry

        lax.fori_loop(1, rows, shared, 0)


def per_device(mesh, pair_input, saved_product, pair_grad, token_mask, *weights):
    rows = mesh.shape["row"]
    n_col, n_ch = mesh.shape["col"], mesh.shape["ch"]
    tr, tc, width = pair_input.shape
    pairs = tr * tc
    tokens = token_mask.shape[0]
    hid = weights[0].shape[1]
    chunk = 288 if pairs % 288 == 0 else pairs
    ktile = 24 if tc % 24 == 0 else tc
    n_k, n_z = n_col * n_ch, rows // 2
    flat = [array.reshape(pairs, width) for array in (pair_input, saved_product, pair_grad)]
    arrays = [*flat, token_mask.reshape(1, tokens), *weights]
    vmem = pltpu.VMEM
    dma = pltpu.SemaphoreType.DMA
    tile32 = vmem((pairs, width), f32)
    sizes = (rows, pairs, tr, tc, tokens, n_col, n_ch, chunk, ktile)
    out = pl.pallas_call(
        functools.partial(kernel, sizes),
        out_shape=pltpu.VMEM((pairs, width), f32),
        in_specs=[pl.BlockSpec(memory_space=pl.ANY)] * 13,
        out_specs=pl.BlockSpec(memory_space=vmem),
        scratch_shapes=[
            vmem((3 * width, 2 * hid), bf16),
            vmem((hid, 3 * width), bf16),
            vmem((3 * width, 4 * width), bf16),
            vmem((2 * width, 4 * width), bf16),
            vmem((2 * width, 2 * width), bf16),
            vmem((2 * width, 2 * width), bf16),
            vmem((pairs, hid), f32),
            vmem((pairs, hid), f32),
            tile32,
            tile32,
            vmem((pairs, width), bf16),
            *([tile32] * 9),
            vmem((rows, tr * tr, width), f32),
            vmem((tr * tr, width), f32),
            vmem((rows, pairs, width), f32),
            vmem((rows, pairs, width), bf16),
            vmem((rows, tr * tr, width), bf16),
            vmem((rows, tr * tr, width), bf16),
            dma((2 * n_z,)),
            dma((rows,)),
            dma((2 * n_z,)),
            dma((n_col,)),
            dma((n_ch, n_k)),
            dma((n_k,)),
            dma((rows,)),
            dma((rows,)),
            dma((n_ch, rows)),
            dma((13,)),
            *[vmem(array.shape, array.dtype) for array in arrays],
        ],
        compiler_params=pltpu.CompilerParams(
            collective_id=0, has_side_effects=True, vmem_limit_bytes=60 * 1024 * 1024
        ),
    )(*arrays)
    return out.reshape(tr, tc, width)


def solution(mesh):
    tile = P(("grp", "row"), ("col", "ch"), None)
    in_specs = (tile, tile, tile, P("grp")) + (P(),) * 9
    return jax.shard_map(
        functools.partial(per_device, mesh), mesh=mesh, in_specs=in_specs, out_specs=tile, check_vma=False
    )
```

```python
import functools

import jax
import jax.numpy as jnp
from jax import lax
from jax.experimental import pallas as pl
from jax.experimental.pallas import tpu as pltpu
from jax.sharding import PartitionSpec as P

epsilon = 1e-05
f32 = jnp.float32
bf16 = jnp.bfloat16
MESH = pl.DeviceIdType.MESH


def split(values):
    high = values.astype(bf16)
    return high, (values - high.astype(f32)).astype(bf16)


def dot(values, weights, transposed=False):
    dims = (((1,), (1 if transposed else 0,)), ((), ()))
    return lax.dot_general(values, weights, dimension_numbers=dims, preferred_element_type=f32)


def fold_halves(values):
    half = values.shape[1] // 2
    return values[:, :half] + values[:, half:]


def both_parts(values):
    return jnp.concatenate(split(values), axis=1)


def sigmoid(values):
    return 0.5 * jnp.tanh(0.5 * values) + 0.5


def normalize(values):
    center = values - jnp.mean(values, axis=-1, keepdims=True)
    inv_std = lax.rsqrt(jnp.mean(center * center, axis=-1, keepdims=True) + epsilon)
    return (center * inv_std, inv_std)


def norm_back(normed, inv_std, upstream):
    mean_up = jnp.mean(upstream, axis=-1, keepdims=True)
    mean_proj = jnp.mean(upstream * normed, axis=-1, keepdims=True)
    return (upstream - mean_up - normed * mean_proj) * inv_std


def kernel(
    sizes,
    x_in,
    s_in,
    g_in,
    mask_in,
    w1_in,
    w2_in,
    w3_in,
    wl_in,
    wlg_in,
    wr_in,
    wrg_in,
    wo_in,
    wog_in,
    out_ref,
    w12x,
    w3x,
    w5x,
    w4x,
    wogx,
    wox,
    h1s,
    h2s,
    nms,
    ims,
    nos,
    lgm,
    lq,
    rgm,
    rq,
    gts,
    masks,
    right32,
    accl,
    accr,
    gp32,
    gpt32,
    left_all,
    nm_all,
    gp_row,
    gpt,
    nm_send,
    nm_recv,
    fw_send,
    gx_send,
    gc_send,
    gp_recv,
    gt_send,
    gt_recv,
    gtf_send,
    in_sem,
    x_ref,
    s_ref,
    g_ref,
    mask_ref,
    w1_ref,
    w2_ref,
    w3_ref,
    wl_ref,
    wlg_ref,
    wr_ref,
    wrg_ref,
    wo_ref,
    wog_ref,
):
    rows, pairs, tr, tc, tokens, n_col, n_ch, chunk, ktile = sizes
    n_z = rows // 2
    ratio = tc // tr
    width = out_ref.shape[1]
    hid = w1_in.shape[1]
    steps = pairs // chunk
    row = lax.axis_index("row")
    my_z, my_y = row // 2, row % 2
    col, ch = lax.axis_index("col"), lax.axis_index("ch")
    my_k = col * n_ch + ch
    y_peer = my_z * 2 + (1 - my_y)

    def z_valid(delta):
        return (my_z + delta >= 0) & (my_z + delta < n_z)

    def z_row(delta):
        return (my_z + delta) * 2 + my_y

    def col_at(dcol):
        return lax.rem(col + dcol, n_col)

    def ch_at(dch):
        return lax.rem(ch + dch, n_ch)

    barrier = pltpu.get_barrier_semaphore()
    for far in range(1, rows):
        pl.semaphore_signal(barrier, inc=1, device_id={"row": lax.rem(row + far, rows)}, device_id_type=MESH)
    for dcol in range(1, n_col):
        pl.semaphore_signal(barrier, inc=1, device_id={"col": col_at(dcol)}, device_id_type=MESH)
    for dch in range(1, n_ch):
        pl.semaphore_signal(barrier, inc=1, device_id={"ch": ch_at(dch)}, device_id_type=MESH)

    inputs = []
    for source, target in (
        (x_in, x_ref),
        (w1_in, w1_ref),
        (w2_in, w2_ref),
        (mask_in, mask_ref),
        (w3_in, w3_ref),
        (wog_in, wog_ref),
        (wo_in, wo_ref),
        (s_in, s_ref),
        (g_in, g_ref),
        (wl_in, wl_ref),
        (wlg_in, wlg_ref),
        (wr_in, wr_ref),
        (wrg_in, wrg_ref),
    ):
        copy = pltpu.make_async_copy(source, target, in_sem.at[len(inputs)])
        copy.start()
        inputs.append(copy)

    def loaded(count):
        for _ in range(count):
            inputs.pop(0).wait()

    def put(source, high_at, low_at):
        high, low = split(source[...])
        for ref, at in high_at:
            ref[at[0] : at[0] + high.shape[0], at[1] : at[1] + high.shape[1]] = high
        ref, at = low_at
        ref[at[0] : at[0] + high.shape[0], at[1] : at[1] + high.shape[1]] = low

    def put_tall(target, source, at):
        put(source, [(target, (0, at)), (target, (width, at))], (target, (2 * width, at)))

    loaded(1)

    def first(step, carry):
        here = pl.ds(pl.multiple_of(step * chunk, chunk), chunk)
        nms[here, :] = normalize(x_ref[here, :])[0]
        return carry

    lax.fori_loop(0, steps, first, 0)
    loaded(4)
    put_tall(w12x, w1_ref, 0)
    put_tall(w12x, w2_ref, hid)
    put(w3_ref, [(w3x, (0, 0)), (w3x, (0, width))], (w3x, (0, 2 * width)))

    def front(step, carry):
        base = pl.multiple_of(step * chunk, chunk)
        here = pl.ds(base, chunk)
        pair_input = x_ref[here, :]
        parts = both_parts(nms[here, :])
        hidden = dot(parts, w12x[: 2 * width, :]) + dot(parts[:, :width], w12x[2 * width :, :])
        hidden_one, hidden_two = hidden[:, :hid], hidden[:, hid:]
        h1s[here, :] = hidden_one
        h2s[here, :] = hidden_two
        act = hidden_one * sigmoid(hidden_one) * hidden_two
        high, low = split(act)
        updated = pair_input + (fold_halves(dot(high, w3x[:, width:])) + dot(low, w3x[:, :width]))
        normed_mid, inv_mid = normalize(updated)
        nms[here, :] = normed_mid
        ims[here, :] = jnp.broadcast_to(inv_mid, (chunk, 128))
        nm_all[row, here, :] = normed_mid.astype(bf16)
        return carry

    lax.fori_loop(0, steps, front, 0)
    pl.semaphore_wait(barrier, rows - 1 + n_col - 1 + n_ch - 1)

    def nm_copy(slot, sem, target):
        return pltpu.make_async_remote_copy(
            src_ref=nm_all.at[slot],
            dst_ref=nm_all.at[slot],
            send_sem=sem,
            recv_sem=nm_recv.at[slot],
            device_id={"row": target},
            device_id_type=MESH,
        )

    sends = []
    held = []

    def start(copy):
        copy.start()
        sends.append(copy)

    def start_if(cond, copy):
        pl.when(cond)(copy.start)
        held.append((cond, copy))

    def slot_copy(slot, sem, target):
        place = gp_row.at[pl.ds(slot * ratio, ratio)]
        return pltpu.make_async_remote_copy(
            src_ref=place,
            dst_ref=place,
            send_sem=sem,
            recv_sem=gp_recv.at[slot],
            device_id=target,
            device_id_type=MESH,
        )

    def piece_copy(target_row):
        return pltpu.make_async_remote_copy(
            src_ref=gp_row.at[target_row],
            dst_ref=gpt.at[row],
            send_sem=gt_send.at[target_row],
            recv_sem=gt_recv.at[row],
            device_id={"row": target_row},
            device_id_type=MESH,
        )

    def share_copy(source_row, dch):
        return pltpu.make_async_remote_copy(
            src_ref=gpt.at[source_row],
            dst_ref=gpt.at[source_row],
            send_sem=gtf_send.at[dch - 1, source_row],
            recv_sem=gt_recv.at[source_row],
            device_id={"ch": ch_at(dch)},
            device_id_type=MESH,
        )

    for far in range(n_z - 1, 0, -1):
        for delta in (far, -far):
            sem = nm_send.at[2 * far - 1 + (delta < 0)]
            start_if(z_valid(delta), nm_copy(row, sem, z_row(delta)))
    start(nm_copy(row, nm_send.at[0], y_peer))

    loaded(4)
    put(wog_ref, [(wogx, (0, 0)), (wogx, (width, 0))], (wogx, (0, width)))
    put(wo_ref, [(wox, (0, 0)), (wox, (0, width))], (wox, (width, 0)))
    wogx[width:, width:] = jnp.zeros((width, width), bf16)
    wox[width:, width:] = jnp.zeros((width, width), bf16)

    token = lax.broadcasted_iota(jnp.int32, (tc, tokens), 1)
    spot = lax.broadcasted_iota(jnp.int32, (tc, tokens), 0)
    mask = mask_ref[...].astype(f32)
    col_mask = jnp.sum(
        jnp.where(token == spot + my_k * tc, jnp.broadcast_to(mask, (tc, tokens)), 0.0), axis=1, keepdims=True
    )
    col_mask = jnp.concatenate([jnp.broadcast_to(col_mask, (tc, 128))] * (chunk // tc), axis=0)

    for step in range(steps):
        base = step * chunk
        here = pl.ds(base, chunk)
        token = lax.broadcasted_iota(jnp.int32, (chunk, tokens), 1)
        spot = lax.broadcasted_iota(jnp.int32, (chunk, tokens), 0) + base
        ahead = spot - (token - row * tr) * tc
        row_mask = jnp.sum(
            jnp.where((ahead >= 0) & (ahead < tc), jnp.broadcast_to(mask, (chunk, tokens)), 0.0), axis=1, keepdims=True
        )
        masks[here, :] = col_mask * row_mask
        out_gate = sigmoid(fold_halves(dot(both_parts(nms[here, :]), wogx[...])))
        pair_grad = g_ref[here, :]
        normed_out, inv_out = normalize(s_ref[here, :])
        nos[here, :] = normed_out.astype(bf16)
        grad_normed = fold_halves(dot(both_parts(pair_grad * out_gate), wox[...], True))
        product = norm_back(normed_out, inv_out, grad_normed).astype(bf16).astype(f32) * masks[here, :]
        gts[here, :] = pair_grad * out_gate * (1.0 - out_gate)
        for i in range(chunk // tc):
            for part in range(ratio):
                at = (step * (chunk // tc) + i) * tr
                gp32[my_k * ratio + part, at : at + tr, :] = product[i * tc + part * tr : i * tc + (part + 1) * tr, :]

    for part in range(ratio):
        gp_row[my_k * ratio + part] = gp32[my_k * ratio + part].astype(bf16)

    def pieces(dcol):
        for part in range(ratio):
            target_row = (col_at(dcol) * n_ch + ch) * ratio + part
            start_if(target_row != row, piece_copy(target_row))

    def gather_share(dcol):
        slot = col_at(dcol) * n_ch + ch
        for dch in range(1, n_ch):
            start(slot_copy(slot, gc_send.at[dch - 1, slot], {"ch": ch_at(dch)}))

    for dcol in range(1, n_col):
        start(slot_copy(my_k, gx_send.at[dcol], {"col": col_at(dcol)}))
    gather_share(0)
    pieces(0)

    loaded(4)
    put_tall(w5x, wl_ref, 0)
    put_tall(w5x, wlg_ref, width)
    put_tall(w5x, wr_ref, 2 * width)
    put_tall(w5x, wrg_ref, 3 * width)
    w4x[...] = w5x[width:, :] * bf16(0.5)

    def own(step, carry):
        here = pl.ds(pl.multiple_of(step * chunk, chunk), chunk)
        parts = both_parts(nms[here, :])
        proj = dot(parts, w5x[: 2 * width, :]) + dot(parts[:, :width], w5x[2 * width :, :])
        left_proj, left_gate = proj[:, :128], sigmoid(proj[:, 128:256])
        right_proj, right_gate = proj[:, 256:384], sigmoid(proj[:, 384:])
        pair_mask = masks[here, :]
        lgm[here, :] = pair_mask * left_gate
        lq[here, :] = left_proj * (1.0 - left_gate)
        rgm[here, :] = pair_mask * right_gate
        rq[here, :] = right_proj * (1.0 - right_gate)
        left_all[row, here, :] = (left_gate * left_proj).astype(bf16).astype(f32)
        right32[here, :] = (right_gate * right_proj).astype(bf16).astype(f32)
        return carry

    lax.fori_loop(0, steps, own, 0)

    def middle(step, carry):
        here = pl.ds(pl.multiple_of(step * 48, 48), 48)
        hidden_one, hidden_two = h1s[here, :], h2s[here, :]
        sig_one = sigmoid(hidden_one)
        h1s[here, :] = hidden_two * sig_one * (1.0 + hidden_one * (1.0 - sig_one))
        h2s[here, :] = hidden_one * sig_one
        return carry

    def gate_back(step, carry):
        here = pl.ds(pl.multiple_of(step * chunk, chunk), chunk)
        gate_term = gts[here, :] * dot(nos[here, :], wox[:width, :width])
        gts[here, :] = dot(gate_term.astype(bf16), wogx[:width, :width], True)
        return carry

    def widen(slot):
        for part in range(ratio):
            gp32[slot * ratio + part] = gp_row[slot * ratio + part].astype(f32)

    k_bases = range(0, tc, ktile)

    def fold_left(owner, first):
        for k_base in k_bases:

            def body(j, acc):
                tile = right32[pl.ds(pl.multiple_of(j * tc + k_base, 8), ktile), :]
                return tuple(acc[i] + gp32[owner, pl.ds(i * tr + j, 1), :] * tile for i in range(tr))

            begin = tuple(
                jnp.zeros((ktile, 128), f32) if first else accl[pl.ds(i * tc + k_base, ktile), :] for i in range(tr)
            )
            acc = lax.fori_loop(0, tr, body, begin, unroll=True)
            for i in range(tr):
                accl[pl.ds(i * tc + k_base, ktile), :] = acc[i]

    def fold_right(source, first):
        if first:
            gpt32[...] = gp32[row]
        else:
            gpt32[...] = gpt[source].astype(f32)
        for k_base in k_bases:

            def body(i, acc):
                tile = left_all[source, pl.ds(pl.multiple_of(i * tc + k_base, 8), ktile), :]
                return tuple(acc[j] + gpt32[pl.ds(i * tr + j, 1), :] * tile for j in range(tr))

            begin = tuple(
                jnp.zeros((ktile, 128), f32) if first else accr[pl.ds(j * tc + k_base, ktile), :] for j in range(tr)
            )
            acc = lax.fori_loop(0, tr, body, begin, unroll=True)
            for j in range(tr):
                accr[pl.ds(j * tc + k_base, ktile), :] = acc[j]

    def block(source):
        def project(step, carry):
            here = pl.ds(pl.multiple_of(step * chunk, chunk), chunk)
            values = nm_all[source, here, :]
            proj = dot(jnp.concatenate([values, values], axis=1), w4x[...])
            left_half, right_half = proj[:, :128], proj[:, 256:384]
            left_all[source, here, :] = left_half * jnp.tanh(proj[:, 128:256]) + left_half
            right32[here, :] = right_half * jnp.tanh(proj[:, 384:]) + right_half
            return carry

        lax.fori_loop(0, steps, project, 0)
        fold_left(source, False)

    lax.fori_loop(0, pairs // 48, middle, 0)
    lax.fori_loop(0, steps, gate_back, 0)

    def delta_of(index):
        return (index // 2 + 1) * (1 - 2 * lax.rem(index, 2))

    partner = (my_z + 1 - 2 * lax.rem(my_z, 2)) * 2 + my_y

    def z_forward(index, carry):
        delta = delta_of(index)
        source = z_row(delta)
        forward = nm_copy(source, fw_send.at[index], y_peer)

        @pl.when(z_valid(delta) & (source != partner))
        def _():
            forward.wait_recv()
            forward.start()

        @pl.when(z_valid(delta) & (source == partner))
        def _():
            forward.wait_recv()

        return carry

    def y_forward():
        forward = nm_copy(y_peer, fw_send.at[2 * n_z - 2], partner)
        forward.wait_recv()
        forward.start()

    def z_block(index, carry):
        delta = delta_of(index)

        @pl.when(z_valid(delta))
        def _():
            block(z_row(delta))

        return carry

    for dcol in range(1, n_col):
        slot = col_at(dcol) * n_ch + ch
        slot_copy(slot, gx_send.at[dcol], {"col": col_at(dcol)}).wait_recv()
        gather_share(dcol)
        pieces(dcol)
        widen(slot)
    for dcol in range(n_col):
        for dch in range(1, n_ch):
            slot = col_at(dcol) * n_ch + ch_at(dch)
            slot_copy(slot, gc_send.at[dch - 1, slot], {"ch": ch_at(dch)}).wait_recv()
            widen(slot)
    fold_left(row, True)
    fold_right(row, True)

    def y_block(source):
        nm_copy(source, fw_send.at[0], y_peer).wait_recv()
        block(source)

    def y_blocks(index, carry):
        delta = delta_of(index)

        @pl.when(z_valid(delta))
        def _():
            y_block((my_z + delta) * 2 + (1 - my_y))

        return carry

    head = lax.rem(row // ratio, n_ch) == ch

    def take(source):
        share_copy(source, 1).wait_recv()

        @pl.when(head)
        def _():
            for dch in range(1, n_ch):
                share_copy(source, dch).start()

    def other_row(delta):
        return (my_z + delta) * 2 + (1 - my_y)

    def over(visit):
        def body(index, carry):
            delta = delta_of(index)
            pl.when(z_valid(delta))(lambda: visit(delta))
            return carry

        lax.fori_loop(0, 2 * n_z - 2, body, 0)

    def z_step(index, carry):
        z_forward(index, carry)
        return z_block(index, carry)

    def rights(far, carry):
        fold_right(lax.rem(row + far, rows), False)
        return carry

    y_forward()
    block(y_peer)
    lax.fori_loop(0, 2 * n_z - 2, z_step, 0)
    y_block(partner + 1 - 2 * my_y)
    take(y_peer)
    over(lambda delta: take(z_row(delta)))
    over(lambda delta: take(other_row(delta)))

    def rest(delta):
        pl.when(z_row(delta) != partner)(lambda: y_block(other_row(delta)))

    over(rest)
    lax.fori_loop(1, rows, rights, 0)

    def back(step, carry):
        here = pl.ds(pl.multiple_of(step * chunk, chunk), chunk)
        left_scaled = accl[here, :] * lgm[here, :]
        right_scaled = accr[here, :] * rgm[here, :]
        wide = jnp.concatenate(
            [left_scaled, left_scaled * lq[here, :], right_scaled, right_scaled * rq[here, :]], axis=1
        )
        high, low = split(wide)
        grad_mid = gts[here, :] + (fold_halves(dot(high, w5x[width:, :], True)) + dot(low, w5x[:width, :], True))
        grad_updated = g_ref[here, :] + norm_back(nms[here, :], ims[here, :], grad_mid)
        grad_hidden = dot(both_parts(grad_updated), w3x[:, : 2 * width], True)
        both = jnp.concatenate([grad_hidden * h1s[here, :], grad_hidden * h2s[here, :]], axis=1)
        grad_normed_in = fold_halves(dot(both.astype(bf16), w12x[width:, :], True))
        normed_in, inv_in = normalize(x_ref[here, :])
        out_ref[here, :] = grad_updated + norm_back(normed_in, inv_in, grad_normed_in)
        return carry

    lax.fori_loop(0, steps, back, 0)

    for copy in sends:
        copy.wait_send()
    for cond, copy in held:
        pl.when(cond)(copy.wait_send)

    def forwarded(index, carry):
        delta = delta_of(index)

        @pl.when(z_valid(delta) & (z_row(delta) != partner))
        def _():
            nm_copy(z_row(delta), fw_send.at[index], y_peer).wait_send()

        return carry

    nm_copy(y_peer, fw_send.at[2 * n_z - 2], partner).wait_send()

    lax.fori_loop(0, 2 * n_z - 2, forwarded, 0)

    @pl.when(head)
    def _():
        def shared(far, carry):
            for dch in range(1, n_ch):
                share_copy(lax.rem(row + far, rows), dch).wait_send()
            return carry

        lax.fori_loop(1, rows, shared, 0)


def per_device(mesh, pair_input, saved_product, pair_grad, token_mask, *weights):
    rows = mesh.shape["row"]
    n_col, n_ch = mesh.shape["col"], mesh.shape["ch"]
    tr, tc, width = pair_input.shape
    pairs = tr * tc
    tokens = token_mask.shape[0]
    hid = weights[0].shape[1]
    chunk = 288 if pairs % 288 == 0 else pairs
    ktile = 24 if tc % 24 == 0 else tc
    n_k, n_z = n_col * n_ch, rows // 2
    flat = [array.reshape(pairs, width) for array in (pair_input, saved_product, pair_grad)]
    arrays = [*flat, token_mask.reshape(1, tokens), *weights]
    vmem = pltpu.VMEM
    dma = pltpu.SemaphoreType.DMA
    tile32 = vmem((pairs, width), f32)
    sizes = (rows, pairs, tr, tc, tokens, n_col, n_ch, chunk, ktile)
    out = pl.pallas_call(
        functools.partial(kernel, sizes),
        out_shape=pltpu.VMEM((pairs, width), f32),
        in_specs=[pl.BlockSpec(memory_space=pl.ANY)] * 13,
        out_specs=pl.BlockSpec(memory_space=vmem),
        scratch_shapes=[
            vmem((3 * width, 2 * hid), bf16),
            vmem((hid, 3 * width), bf16),
            vmem((3 * width, 4 * width), bf16),
            vmem((2 * width, 4 * width), bf16),
            vmem((2 * width, 2 * width), bf16),
            vmem((2 * width, 2 * width), bf16),
            vmem((pairs, hid), f32),
            vmem((pairs, hid), f32),
            tile32,
            tile32,
            vmem((pairs, width), bf16),
            *([tile32] * 9),
            vmem((rows, tr * tr, width), f32),
            vmem((tr * tr, width), f32),
            vmem((rows, pairs, width), f32),
            vmem((rows, pairs, width), bf16),
            vmem((rows, tr * tr, width), bf16),
            vmem((rows, tr * tr, width), bf16),
            dma((2 * n_z,)),
            dma((rows,)),
            dma((2 * n_z,)),
            dma((n_col,)),
            dma((n_ch, n_k)),
            dma((n_k,)),
            dma((rows,)),
            dma((rows,)),
            dma((n_ch, rows)),
            dma((13,)),
            *[vmem(array.shape, array.dtype) for array in arrays],
        ],
        compiler_params=pltpu.CompilerParams(
            collective_id=0, has_side_effects=True, vmem_limit_bytes=60 * 1024 * 1024
        ),
    )(*arrays)
    return out.reshape(tr, tc, width)


def solution(mesh):
    tile = P(("grp", "row"), ("col", "ch"), None)
    in_specs = (tile, tile, tile, P("grp")) + (P(),) * 9
    return jax.shard_map(
        functools.partial(per_device, mesh), mesh=mesh, in_specs=in_specs, out_specs=tile, check_vma=False
    )
```

```python
import functools

import jax
import jax.numpy as jnp
from jax import lax
from jax.experimental import pallas as pl
from jax.experimental.pallas import tpu as pltpu
from jax.sharding import PartitionSpec as P

epsilon = 1e-05
f32 = jnp.float32
bf16 = jnp.bfloat16
MESH = pl.DeviceIdType.MESH


def split(values):
    high = values.astype(bf16)
    return high, (values - high.astype(f32)).astype(bf16)


def dot(values, weights, transposed=False):
    dims = (((1,), (1 if transposed else 0,)), ((), ()))
    return lax.dot_general(values, weights, dimension_numbers=dims, preferred_element_type=f32)


def fold_halves(values):
    half = values.shape[1] // 2
    return values[:, :half] + values[:, half:]


def both_parts(values):
    return jnp.concatenate(split(values), axis=1)


def sigmoid(values):
    return 0.5 * jnp.tanh(0.5 * values) + 0.5


def normalize(values):
    center = values - jnp.mean(values, axis=-1, keepdims=True)
    inv_std = lax.rsqrt(jnp.mean(center * center, axis=-1, keepdims=True) + epsilon)
    return (center * inv_std, inv_std)


def norm_back(normed, inv_std, upstream):
    mean_up = jnp.mean(upstream, axis=-1, keepdims=True)
    mean_proj = jnp.mean(upstream * normed, axis=-1, keepdims=True)
    return (upstream - mean_up - normed * mean_proj) * inv_std


def kernel(
    sizes,
    x_in,
    s_in,
    g_in,
    mask_in,
    w1_in,
    w2_in,
    w3_in,
    wl_in,
    wlg_in,
    wr_in,
    wrg_in,
    wo_in,
    wog_in,
    out_ref,
    w12x,
    w3x,
    w5x,
    w4x,
    wogx,
    wox,
    h1s,
    h2s,
    nms,
    ims,
    nos,
    lgm,
    lq,
    rgm,
    rq,
    gts,
    masks,
    right32,
    accl,
    accr,
    gp32,
    gpt32,
    left_all,
    nm_all,
    gp_row,
    gpt,
    nm_send,
    nm_recv,
    fw_send,
    gx_send,
    gc_send,
    gp_recv,
    gt_send,
    gt_recv,
    gtf_send,
    in_sem,
    x_ref,
    s_ref,
    g_ref,
    mask_ref,
    w1_ref,
    w2_ref,
    w3_ref,
    wl_ref,
    wlg_ref,
    wr_ref,
    wrg_ref,
    wo_ref,
    wog_ref,
):
    rows, pairs, tr, tc, tokens, n_col, n_ch, chunk, ktile = sizes
    n_z = rows // 2
    ratio = tc // tr
    width = out_ref.shape[1]
    hid = w1_in.shape[1]
    steps = pairs // chunk
    row = lax.axis_index("row")
    my_z, my_y = row // 2, row % 2
    col, ch = lax.axis_index("col"), lax.axis_index("ch")
    my_k = col * n_ch + ch
    y_peer = my_z * 2 + (1 - my_y)

    def z_valid(delta):
        return (my_z + delta >= 0) & (my_z + delta < n_z)

    def z_row(delta):
        return (my_z + delta) * 2 + my_y

    def col_at(dcol):
        return lax.rem(col + dcol, n_col)

    def ch_at(dch):
        return lax.rem(ch + dch, n_ch)

    barrier = pltpu.get_barrier_semaphore()
    for far in range(1, rows):
        pl.semaphore_signal(barrier, inc=1, device_id={"row": lax.rem(row + far, rows)}, device_id_type=MESH)
    for dcol in range(1, n_col):
        pl.semaphore_signal(barrier, inc=1, device_id={"col": col_at(dcol)}, device_id_type=MESH)
    for dch in range(1, n_ch):
        pl.semaphore_signal(barrier, inc=1, device_id={"ch": ch_at(dch)}, device_id_type=MESH)

    inputs = []
    for source, target in (
        (x_in, x_ref),
        (w1_in, w1_ref),
        (w2_in, w2_ref),
        (mask_in, mask_ref),
        (w3_in, w3_ref),
        (wog_in, wog_ref),
        (wo_in, wo_ref),
        (s_in, s_ref),
        (g_in, g_ref),
        (wl_in, wl_ref),
        (wlg_in, wlg_ref),
        (wr_in, wr_ref),
        (wrg_in, wrg_ref),
    ):
        copy = pltpu.make_async_copy(source, target, in_sem.at[len(inputs)])
        copy.start()
        inputs.append(copy)

    def loaded(count):
        for _ in range(count):
            inputs.pop(0).wait()

    def put(source, high_at, low_at):
        high, low = split(source[...])
        for ref, at in high_at:
            ref[at[0] : at[0] + high.shape[0], at[1] : at[1] + high.shape[1]] = high
        ref, at = low_at
        ref[at[0] : at[0] + high.shape[0], at[1] : at[1] + high.shape[1]] = low

    def put_tall(target, source, at):
        put(source, [(target, (0, at)), (target, (width, at))], (target, (2 * width, at)))

    loaded(1)

    def first(step, carry):
        here = pl.ds(pl.multiple_of(step * chunk, chunk), chunk)
        nms[here, :] = normalize(x_ref[here, :])[0]
        return carry

    lax.fori_loop(0, steps, first, 0)
    loaded(4)
    put_tall(w12x, w1_ref, 0)
    put_tall(w12x, w2_ref, hid)
    put(w3_ref, [(w3x, (0, 0)), (w3x, (0, width))], (w3x, (0, 2 * width)))

    def front(step, carry):
        base = pl.multiple_of(step * chunk, chunk)
        here = pl.ds(base, chunk)
        pair_input = x_ref[here, :]
        parts = both_parts(nms[here, :])
        hidden = dot(parts, w12x[: 2 * width, :]) + dot(parts[:, :width], w12x[2 * width :, :])
        hidden_one, hidden_two = hidden[:, :hid], hidden[:, hid:]
        h1s[here, :] = hidden_one
        h2s[here, :] = hidden_two
        act = hidden_one * sigmoid(hidden_one) * hidden_two
        high, low = split(act)
        updated = pair_input + (fold_halves(dot(high, w3x[:, width:])) + dot(low, w3x[:, :width]))
        normed_mid, inv_mid = normalize(updated)
        nms[here, :] = normed_mid
        ims[here, :] = jnp.broadcast_to(inv_mid, (chunk, 128))
        nm_all[row, here, :] = normed_mid.astype(bf16)
        return carry

    lax.fori_loop(0, steps, front, 0)
    pl.semaphore_wait(barrier, rows - 1 + n_col - 1 + n_ch - 1)

    def nm_copy(slot, sem, target):
        return pltpu.make_async_remote_copy(
            src_ref=nm_all.at[slot],
            dst_ref=nm_all.at[slot],
            send_sem=sem,
            recv_sem=nm_recv.at[slot],
            device_id={"row": target},
            device_id_type=MESH,
        )

    sends = []
    held = []

    def start(copy):
        copy.start()
        sends.append(copy)

    def start_if(cond, copy):
        pl.when(cond)(copy.start)
        held.append((cond, copy))

    def slot_copy(slot, sem, target):
        place = gp_row.at[pl.ds(slot * ratio, ratio)]
        return pltpu.make_async_remote_copy(
            src_ref=place,
            dst_ref=place,
            send_sem=sem,
            recv_sem=gp_recv.at[slot],
            device_id=target,
            device_id_type=MESH,
        )

    def piece_copy(target_row):
        return pltpu.make_async_remote_copy(
            src_ref=gp_row.at[target_row],
            dst_ref=gpt.at[row],
            send_sem=gt_send.at[target_row],
            recv_sem=gt_recv.at[row],
            device_id={"row": target_row},
            device_id_type=MESH,
        )

    def share_copy(source_row, dch):
        return pltpu.make_async_remote_copy(
            src_ref=gpt.at[source_row],
            dst_ref=gpt.at[source_row],
            send_sem=gtf_send.at[dch - 1, source_row],
            recv_sem=gt_recv.at[source_row],
            device_id={"ch": ch_at(dch)},
            device_id_type=MESH,
        )

    for far in range(n_z - 1, 0, -1):
        for delta in (far, -far):
            sem = nm_send.at[2 * far - 1 + (delta < 0)]
            start_if(z_valid(delta), nm_copy(row, sem, z_row(delta)))
    start(nm_copy(row, nm_send.at[0], y_peer))

    loaded(4)
    put(wog_ref, [(wogx, (0, 0)), (wogx, (width, 0))], (wogx, (0, width)))
    put(wo_ref, [(wox, (0, 0)), (wox, (0, width))], (wox, (width, 0)))
    wogx[width:, width:] = jnp.zeros((width, width), bf16)
    wox[width:, width:] = jnp.zeros((width, width), bf16)

    token = lax.broadcasted_iota(jnp.int32, (tc, tokens), 1)
    spot = lax.broadcasted_iota(jnp.int32, (tc, tokens), 0)
    mask = mask_ref[...].astype(f32)
    col_mask = jnp.sum(
        jnp.where(token == spot + my_k * tc, jnp.broadcast_to(mask, (tc, tokens)), 0.0), axis=1, keepdims=True
    )
    col_mask = jnp.concatenate([jnp.broadcast_to(col_mask, (tc, 128))] * (chunk // tc), axis=0)

    for step in range(steps):
        base = step * chunk
        here = pl.ds(base, chunk)
        token = lax.broadcasted_iota(jnp.int32, (chunk, tokens), 1)
        spot = lax.broadcasted_iota(jnp.int32, (chunk, tokens), 0) + base
        ahead = spot - (token - row * tr) * tc
        row_mask = jnp.sum(
            jnp.where((ahead >= 0) & (ahead < tc), jnp.broadcast_to(mask, (chunk, tokens)), 0.0), axis=1, keepdims=True
        )
        masks[here, :] = col_mask * row_mask
        out_gate = sigmoid(fold_halves(dot(both_parts(nms[here, :]), wogx[...])))
        pair_grad = g_ref[here, :]
        normed_out, inv_out = normalize(s_ref[here, :])
        nos[here, :] = normed_out.astype(bf16)
        grad_normed = fold_halves(dot(both_parts(pair_grad * out_gate), wox[...], True))
        product = norm_back(normed_out, inv_out, grad_normed).astype(bf16).astype(f32) * masks[here, :]
        gts[here, :] = pair_grad * out_gate * (1.0 - out_gate)
        for i in range(chunk // tc):
            for part in range(ratio):
                at = (step * (chunk // tc) + i) * tr
                gp32[my_k * ratio + part, at : at + tr, :] = product[i * tc + part * tr : i * tc + (part + 1) * tr, :]

    for part in range(ratio):
        gp_row[my_k * ratio + part] = gp32[my_k * ratio + part].astype(bf16)

    def pieces(dcol):
        for part in range(ratio):
            target_row = (col_at(dcol) * n_ch + ch) * ratio + part
            start_if(target_row != row, piece_copy(target_row))

    def gather_share(dcol):
        slot = col_at(dcol) * n_ch + ch
        for dch in range(1, n_ch):
            start(slot_copy(slot, gc_send.at[dch - 1, slot], {"ch": ch_at(dch)}))

    for dcol in range(1, n_col):
        start(slot_copy(my_k, gx_send.at[dcol], {"col": col_at(dcol)}))
    gather_share(0)
    pieces(0)

    loaded(4)
    put_tall(w5x, wl_ref, 0)
    put_tall(w5x, wlg_ref, width)
    put_tall(w5x, wr_ref, 2 * width)
    put_tall(w5x, wrg_ref, 3 * width)
    w4x[...] = w5x[width:, :] * bf16(0.5)

    def own(step, carry):
        here = pl.ds(pl.multiple_of(step * chunk, chunk), chunk)
        parts = both_parts(nms[here, :])
        proj = dot(parts, w5x[: 2 * width, :]) + dot(parts[:, :width], w5x[2 * width :, :])
        left_proj, left_gate = proj[:, :128], sigmoid(proj[:, 128:256])
        right_proj, right_gate = proj[:, 256:384], sigmoid(proj[:, 384:])
        pair_mask = masks[here, :]
        lgm[here, :] = pair_mask * left_gate
        lq[here, :] = left_proj * (1.0 - left_gate)
        rgm[here, :] = pair_mask * right_gate
        rq[here, :] = right_proj * (1.0 - right_gate)
        left_all[row, here, :] = (left_gate * left_proj).astype(bf16).astype(f32)
        right32[here, :] = (right_gate * right_proj).astype(bf16).astype(f32)
        return carry

    lax.fori_loop(0, steps, own, 0)

    def middle(step, carry):
        here = pl.ds(pl.multiple_of(step * 48, 48), 48)
        hidden_one, hidden_two = h1s[here, :], h2s[here, :]
        sig_one = sigmoid(hidden_one)
        h1s[here, :] = hidden_two * sig_one * (1.0 + hidden_one * (1.0 - sig_one))
        h2s[here, :] = hidden_one * sig_one
        return carry

    def gate_back(step, carry):
        here = pl.ds(pl.multiple_of(step * chunk, chunk), chunk)
        gate_term = gts[here, :] * dot(nos[here, :], wox[:width, :width])
        gts[here, :] = dot(gate_term.astype(bf16), wogx[:width, :width], True)
        return carry

    def widen(slot):
        for part in range(ratio):
            gp32[slot * ratio + part] = gp_row[slot * ratio + part].astype(f32)

    k_bases = range(0, tc, ktile)

    def fold_left(owner, first):
        for k_base in k_bases:

            def body(j, acc):
                tile = right32[pl.ds(pl.multiple_of(j * tc + k_base, 8), ktile), :]
                return tuple(acc[i] + gp32[owner, pl.ds(i * tr + j, 1), :] * tile for i in range(tr))

            begin = tuple(
                jnp.zeros((ktile, 128), f32) if first else accl[pl.ds(i * tc + k_base, ktile), :] for i in range(tr)
            )
            acc = lax.fori_loop(0, tr, body, begin, unroll=True)
            for i in range(tr):
                accl[pl.ds(i * tc + k_base, ktile), :] = acc[i]

    def fold_right(source, first):
        if first:
            gpt32[...] = gp32[row]
        else:
            gpt32[...] = gpt[source].astype(f32)
        for k_base in k_bases:

            def body(i, acc):
                tile = left_all[source, pl.ds(pl.multiple_of(i * tc + k_base, 8), ktile), :]
                return tuple(acc[j] + gpt32[pl.ds(i * tr + j, 1), :] * tile for j in range(tr))

            begin = tuple(
                jnp.zeros((ktile, 128), f32) if first else accr[pl.ds(j * tc + k_base, ktile), :] for j in range(tr)
            )
            acc = lax.fori_loop(0, tr, body, begin, unroll=True)
            for j in range(tr):
                accr[pl.ds(j * tc + k_base, ktile), :] = acc[j]

    def block(source):
        def project(step, carry):
            here = pl.ds(pl.multiple_of(step * chunk, chunk), chunk)
            values = nm_all[source, here, :]
            proj = dot(jnp.concatenate([values, values], axis=1), w4x[...])
            left_half, right_half = proj[:, :128], proj[:, 256:384]
            left_all[source, here, :] = left_half * jnp.tanh(proj[:, 128:256]) + left_half
            right32[here, :] = right_half * jnp.tanh(proj[:, 384:]) + right_half
            return carry

        lax.fori_loop(0, steps, project, 0)
        fold_left(source, False)

    lax.fori_loop(0, pairs // 48, middle, 0)
    lax.fori_loop(0, steps, gate_back, 0)

    def delta_of(index):
        return (index // 2 + 1) * (1 - 2 * lax.rem(index, 2))

    partner = (my_z + 1 - 2 * lax.rem(my_z, 2)) * 2 + my_y

    def z_forward(index, carry):
        delta = delta_of(index)
        source = z_row(delta)
        forward = nm_copy(source, fw_send.at[index], y_peer)

        @pl.when(z_valid(delta) & (source != partner))
        def _():
            forward.wait_recv()
            forward.start()

        @pl.when(z_valid(delta) & (source == partner))
        def _():
            forward.wait_recv()

        return carry

    def y_forward():
        forward = nm_copy(y_peer, fw_send.at[2 * n_z - 2], partner)
        forward.wait_recv()
        forward.start()

    def z_block(index, carry):
        delta = delta_of(index)

        @pl.when(z_valid(delta))
        def _():
            block(z_row(delta))

        return carry

    for dcol in range(1, n_col):
        slot = col_at(dcol) * n_ch + ch
        slot_copy(slot, gx_send.at[dcol], {"col": col_at(dcol)}).wait_recv()
        gather_share(dcol)
        pieces(dcol)
        widen(slot)
    for dcol in range(n_col):
        for dch in range(1, n_ch):
            slot = col_at(dcol) * n_ch + ch_at(dch)
            slot_copy(slot, gc_send.at[dch - 1, slot], {"ch": ch_at(dch)}).wait_recv()
            widen(slot)
    fold_left(row, True)
    fold_right(row, True)

    def y_block(source):
        nm_copy(source, fw_send.at[0], y_peer).wait_recv()
        block(source)

    def y_blocks(index, carry):
        delta = delta_of(index)

        @pl.when(z_valid(delta))
        def _():
            y_block((my_z + delta) * 2 + (1 - my_y))

        return carry

    head = lax.rem(row // ratio, n_ch) == ch

    def take(source):
        share_copy(source, 1).wait_recv()

        @pl.when(head)
        def _():
            for dch in range(1, n_ch):
                share_copy(source, dch).start()

    def other_row(delta):
        return (my_z + delta) * 2 + (1 - my_y)

    def over(visit):
        def body(index, carry):
            delta = delta_of(index)
            pl.when(z_valid(delta))(lambda: visit(delta))
            return carry

        lax.fori_loop(0, 2 * n_z - 2, body, 0)

    def z_step(index, carry):
        z_forward(index, carry)
        return z_block(index, carry)

    def rights(far, carry):
        fold_right(lax.rem(row + far, rows), False)
        return carry

    y_forward()
    block(y_peer)
    lax.fori_loop(0, 2 * n_z - 2, z_step, 0)
    partner_other = partner + 1 - 2 * my_y

    def rest(delta):
        pl.when(z_row(delta) != partner)(lambda: y_block(other_row(delta)))

    y_block(partner_other)
    pl.when(jnp.logical_not(head))(lambda: over(rest))
    take(y_peer)
    over(lambda delta: take(z_row(delta)))
    over(lambda delta: take(other_row(delta)))
    pl.when(head)(lambda: over(rest))
    lax.fori_loop(1, rows, rights, 0)

    def back(step, carry):
        here = pl.ds(pl.multiple_of(step * chunk, chunk), chunk)
        left_scaled = accl[here, :] * lgm[here, :]
        right_scaled = accr[here, :] * rgm[here, :]
        wide = jnp.concatenate(
            [left_scaled, left_scaled * lq[here, :], right_scaled, right_scaled * rq[here, :]], axis=1
        )
        high, low = split(wide)
        grad_mid = gts[here, :] + (fold_halves(dot(high, w5x[width:, :], True)) + dot(low, w5x[:width, :], True))
        grad_updated = g_ref[here, :] + norm_back(nms[here, :], ims[here, :], grad_mid)
        grad_hidden = dot(both_parts(grad_updated), w3x[:, : 2 * width], True)
        both = jnp.concatenate([grad_hidden * h1s[here, :], grad_hidden * h2s[here, :]], axis=1)
        grad_normed_in = fold_halves(dot(both.astype(bf16), w12x[width:, :], True))
        normed_in, inv_in = normalize(x_ref[here, :])
        out_ref[here, :] = grad_updated + norm_back(normed_in, inv_in, grad_normed_in)
        return carry

    lax.fori_loop(0, steps, back, 0)

    for copy in sends:
        copy.wait_send()
    for cond, copy in held:
        pl.when(cond)(copy.wait_send)

    def forwarded(index, carry):
        delta = delta_of(index)

        @pl.when(z_valid(delta) & (z_row(delta) != partner))
        def _():
            nm_copy(z_row(delta), fw_send.at[index], y_peer).wait_send()

        return carry

    nm_copy(y_peer, fw_send.at[2 * n_z - 2], partner).wait_send()

    lax.fori_loop(0, 2 * n_z - 2, forwarded, 0)

    @pl.when(head)
    def _():
        def shared(far, carry):
            for dch in range(1, n_ch):
                share_copy(lax.rem(row + far, rows), dch).wait_send()
            return carry

        lax.fori_loop(1, rows, shared, 0)


def per_device(mesh, pair_input, saved_product, pair_grad, token_mask, *weights):
    rows = mesh.shape["row"]
    n_col, n_ch = mesh.shape["col"], mesh.shape["ch"]
    tr, tc, width = pair_input.shape
    pairs = tr * tc
    tokens = token_mask.shape[0]
    hid = weights[0].shape[1]
    chunk = 288 if pairs % 288 == 0 else pairs
    ktile = 24 if tc % 24 == 0 else tc
    n_k, n_z = n_col * n_ch, rows // 2
    flat = [array.reshape(pairs, width) for array in (pair_input, saved_product, pair_grad)]
    arrays = [*flat, token_mask.reshape(1, tokens), *weights]
    vmem = pltpu.VMEM
    dma = pltpu.SemaphoreType.DMA
    tile32 = vmem((pairs, width), f32)
    sizes = (rows, pairs, tr, tc, tokens, n_col, n_ch, chunk, ktile)
    out = pl.pallas_call(
        functools.partial(kernel, sizes),
        out_shape=pltpu.VMEM((pairs, width), f32),
        in_specs=[pl.BlockSpec(memory_space=pl.ANY)] * 13,
        out_specs=pl.BlockSpec(memory_space=vmem),
        scratch_shapes=[
            vmem((3 * width, 2 * hid), bf16),
            vmem((hid, 3 * width), bf16),
            vmem((3 * width, 4 * width), bf16),
            vmem((2 * width, 4 * width), bf16),
            vmem((2 * width, 2 * width), bf16),
            vmem((2 * width, 2 * width), bf16),
            vmem((pairs, hid), f32),
            vmem((pairs, hid), f32),
            tile32,
            tile32,
            vmem((pairs, width), bf16),
            *([tile32] * 9),
            vmem((rows, tr * tr, width), f32),
            vmem((tr * tr, width), f32),
            vmem((rows, pairs, width), f32),
            vmem((rows, pairs, width), bf16),
            vmem((rows, tr * tr, width), bf16),
            vmem((rows, tr * tr, width), bf16),
            dma((2 * n_z,)),
            dma((rows,)),
            dma((2 * n_z,)),
            dma((n_col,)),
            dma((n_ch, n_k)),
            dma((n_k,)),
            dma((rows,)),
            dma((rows,)),
            dma((n_ch, rows)),
            dma((13,)),
            *[vmem(array.shape, array.dtype) for array in arrays],
        ],
        compiler_params=pltpu.CompilerParams(
            collective_id=0, has_side_effects=True, vmem_limit_bytes=60 * 1024 * 1024
        ),
    )(*arrays)
    return out.reshape(tr, tc, width)


def solution(mesh):
    tile = P(("grp", "row"), ("col", "ch"), None)
    in_specs = (tile, tile, tile, P("grp")) + (P(),) * 9
    return jax.shard_map(
        functools.partial(per_device, mesh), mesh=mesh, in_specs=in_specs, out_specs=tile, check_vma=False
    )
```
